128 devices in a mesh: row: 16 (over z, x_lo, core), col: 8 (over x_hi, y).
Axes of the slice: x: 4 (x_hi: 2, x_lo: 2; x = x_hi * 2 + x_lo), y: 4, z: 4, core: 2. Of those that a mesh axis runs over, the one named last changes fastest.
Arguments:
- base_weight: bfloat16 [16384, 49152], P('row', 'col'), may hold values from -6 to 6
- left_factor: float32 [16384, 256], P('row', 'col'), may hold values from -6 to 6
- right_factor: float32 [256, 49152], P('row', 'col'), may hold values from -0.375 to 0.375
Outputs:
- merged: bfloat16 [16384, 49152], P(None, ('row', 'col'))
The draws below stay inside these ranges and needn't reach their ends.
All inputs are finite; a program needn't handle non-finite values.
Results may differ from the reference program's by a relative error of at most 0.001.
Values may be sent and summed in bfloat16 or wider, within the bound.
No kernel may reach another device: no remote copies, remote signals or barrier semaphores. Data moves between devices by JAX's collectives and lax.ppermute only.
A program may use at most 192 MiB of HBM per device.

```python
import jax
import jax.numpy as jnp
from jax import lax

D = 16384
FF = 49152
RANK = 256
N_ROW = 16


def steps_of(stream_key, shape, pieces, least, high):
    loudness = 1.0
    for dim, parts in pieces:
        draws = jax.random.uniform(jax.random.fold_in(jax.random.fold_in(stream_key, 6), dim), (parts,), jnp.float32, least / len(pieces), high / len(pieces))
        loudness = loudness * jnp.repeat(jnp.exp(draws), shape[dim] // parts).reshape((-1,) + (1,) * (len(shape) - 1 - dim))
    return loudness


def centred(key, shape, spread, most, split=(), dtype=jnp.bfloat16):
    result = jax.random.normal(key, shape, jnp.float32) * spread
    if len(split) > 0:
        result = steps_of(key, shape, split, -0.22, 0.18) * result
    return jnp.clip(result, min=-most, max=most).astype(dtype)


def setup_inputs(seed: int = 0) -> dict:
    key_list = jax.random.split(jax.random.key(seed), 4)
    base_weight = centred(key_list[0], (D, FF), 1.0, 6.0, ((0, 16), (1, 8)))
    left_factor = centred(key_list[1], (D, RANK), 1.0, 6.0, ((0, 16), (1, 8)), jnp.float32)
    right_factor = centred(key_list[2], (RANK, FF), RANK ** -0.5, 0.375, ((0, 16), (1, 8)), jnp.float32)
    return {"base_weight": base_weight, "left_factor": left_factor, "right_factor": right_factor}


def reference(base_weight, left_factor, right_factor):
    left_blocks = left_factor.reshape(N_ROW, D // N_ROW, RANK)
    base_blocks = base_weight.reshape(N_ROW, D // N_ROW, FF)

    def merge_block(pair):
        left_block, base_block = pair
        delta = jnp.dot(left_block, right_factor, precision=lax.Precision.HIGHEST, preferred_element_type=jnp.float32)
        return (base_block.astype(jnp.float32) + delta).astype(jnp.bfloat16)

    merged = lax.map(merge_block, (left_blocks, base_blocks))
    return merged.reshape(D, FF)
```

```python
import jax
import jax.numpy as jnp
from jax import lax
from jax.sharding import Mesh
from jax.sharding import PartitionSpec as P

AXES = ("z", "xl", "c", "xh", "y")
SIZES = (4, 2, 2, 2, 4)
CHUNKS = 4


def split(value):
    high = lax.reduce_precision(value, 8, 7)
    return high.astype(jnp.bfloat16), (value - high).astype(jnp.bfloat16)


def number(z, xl, c, xh, y):
    return (((z * 2 + xl) * 2 + c) * 2 + xh) * 4 + y


def target(k, z, xl, c, xh):
    k2, k1, k0 = k >> 2, (k >> 1) & 1, k & 1
    return (z >> 1) ^ k2 ^ c, xl ^ k1, xh * 2 + ((z & 1) ^ k0)


def pairs(k):
    out = []
    for z in range(4):
        for xl in range(2):
            for c in range(2):
                for xh in range(2):
                    for y in range(4):
                        xh2, xl2, z2 = target(k, z, xl, c, xh)
                        out.append((number(z, xl, c, xh, y), number(z2, xl2, c, xh2, y)))
    return out


def body(base, left, right):
    height, width = base.shape
    block = width // 16
    rows = height // CHUNKS
    depth = right.shape[0]
    z, xl, c = (lax.axis_index(n) for n in ("z", "xl", "c"))

    lefts = jnp.stack(split(left))
    lefts = lax.all_gather(lefts, ("c", "xh", "y"), axis=0)
    lefts = lefts.reshape(2, 8, 2, height, left.shape[1])
    lefts = lefts.transpose(2, 0, 3, 1, 4).reshape(2, 2, height, 8 * left.shape[1])
    left_cat = jnp.concatenate([lefts[0], lefts[0], lefts[1]], -1)

    rights = jnp.stack(split(right))
    rights = rights.reshape(2, depth, 2, 2, 4, block).transpose(2, 4, 0, 1, 3, 5)
    rights = rights.reshape(8, 2, depth, 2, block)
    rights = lax.all_to_all(rights, ("c", "y"), 0, 0, tiled=True)
    rights = lax.all_gather(rights, ("z", "xl"), axis=0)
    rights = rights.reshape(8, 2, 4, 2, depth, 2, block).transpose(2, 5, 3, 0, 1, 4, 6)
    rights = rights.reshape(4, 2, 2, 16 * depth, block)
    right_cat = jnp.concatenate([rights[:, :, 0], rights[:, :, 1], rights[:, :, 0]], 2)

    order = []
    for k in range(8):
        k2, k1, k0 = k >> 2, (k >> 1) & 1, k & 1
        order.append((((z & 1) ^ k0) * 2 + (xl ^ k1), (z >> 1) ^ k2 ^ c))
    right_cat = jnp.concatenate(
        [lax.dynamic_slice(right_cat, (y, j2, 0, 0), (1, 1, *right_cat.shape[2:]))[0, 0] for y, j2 in order],
        1,
    )

    def first(part):
        part = part.reshape(rows, 2, 2, 4, block).transpose(1, 3, 2, 0, 4)
        part = lax.all_to_all(
            part.reshape(8, 2, rows, block), ("c", "y"), 0, 0, tiled=True
        )
        return part.reshape(2, 4, 2, rows, block)

    def add(i, part):
        part = jnp.concatenate(
            [lax.dynamic_slice(part, (0, y, j2, 0, 0), (2, 1, 1, rows, block))[:, 0, 0] for y, j2 in order],
            2,
        )
        delta = jnp.dot(
            left_cat[:, i * rows : (i + 1) * rows].reshape(2 * rows, -1),
            right_cat,
            preferred_element_type=jnp.float32,
        )
        sent = part.astype(jnp.float32) + delta.reshape(2, rows, 8 * block)
        sent = sent.astype(jnp.bfloat16)
        return [sent[..., k * block : (k + 1) * block] for k in range(8)]

    xh = lax.axis_index("xh")
    merged = jnp.zeros((8, 2, CHUNKS, rows, block), jnp.bfloat16)
    parts = [base[i * rows : (i + 1) * rows] for i in range(CHUNKS)]
    got, sent = [], add(0, first(parts[0]))
    for i in range(CHUNKS):
        if i + 1 < CHUNKS:
            got, sent, parts[i + 1] = lax.optimization_barrier((got, sent, parts[i + 1]))
        else:
            got, sent = lax.optimization_barrier((got, sent))
        arrived = first(parts[i + 1]) if i + 1 < CHUNKS else None
        new = [lax.ppermute(sent[k], AXES, pairs(k)) for k in range(8)]
        for k, one in enumerate(got):
            merged = place(merged, one, i - 1, k, z, xl, c, xh)
        got = new
        if arrived is not None:
            sent = add(i + 1, arrived)
    for k, one in enumerate(got):
        merged = place(merged, one, CHUNKS - 1, k, z, xl, c, xh)
    return merged.reshape(16 * height, block)


def place(merged, one, i, k, z, xl, c, xh):
    k2, k1, k0 = k >> 2, (k >> 1) & 1, k & 1
    slot = ((xh ^ k2 ^ c) * 2 + ((z & 1) ^ k0)) * 2 + (xl ^ k1)
    return lax.dynamic_update_slice(merged, one[None, :, None], (slot, 0, i, 0, 0))


def solution(mesh):
    fine = Mesh(mesh.devices.reshape(SIZES), AXES)
    placed = P(("z", "xl", "c"), ("xh", "y"))
    return jax.shard_map(
        body,
        mesh=fine,
        in_specs=(placed, placed, placed),
        out_specs=P(None, AXES),
        check_vma=False,
    )
```

```python
import functools

import jax
import jax.numpy as jnp
from jax import lax
from jax.experimental import pallas as pl
from jax.experimental.pallas import tpu as pltpu
from jax.sharding import Mesh
from jax.sharding import PartitionSpec as P

AXES = ("z", "xl", "c", "xh", "y")
SIZES = (4, 2, 2, 2, 4)
CHUNKS = 4
AHEAD = 5
VMEM = 60 << 20
ANY = pl.BlockSpec(memory_space=pl.ANY)
SMEM = pl.BlockSpec(memory_space=pltpu.SMEM)
BF16 = jnp.bfloat16


def split(value):
    high = lax.reduce_precision(value, 8, 7)
    return high.astype(BF16), (value - high).astype(BF16)


def number(z, xl, c, xh, y):
    return (((z * 2 + xl) * 2 + c) * 2 + xh) * 4 + y


def bits(k):
    return k >> 2, (k >> 1) & 1, k & 1


def pairs(k):
    k2, k1, k0 = bits(k)
    out = []
    for z in range(4):
        for xl in range(2):
            for c in range(2):
                for xh in range(2):
                    for y in range(4):
                        xh2, xl2 = (z >> 1) ^ k2 ^ c, xl ^ k1
                        z2 = xh * 2 + ((z & 1) ^ k0)
                        out.append((number(z, xl, c, xh, y), number(z2, xl2, c, xh2, y)))
    return out


def moved(change):
    out = []
    for z in range(4):
        for xl in range(2):
            for c in range(2):
                for xh in range(2):
                    for y in range(4):
                        out.append((number(z, xl, c, xh, y), number(*change(z, xl, c, xh, y))))
    return out


def start_all(copies):
    for one in copies:
        one.start()
    return copies


def wait_all(copies):
    for one in copies:
        one.wait()


def pack_kernel(i, rows, block, base, out, buf, sems):
    incoming, outgoing = [], []
    for n in range(16):
        c, y, j = n >> 3, (n >> 1) & 3, n & 1
        column = (c * 8 + j * 4 + y) * block
        source = base.at[pl.ds(i * rows, rows), pl.ds(column, block)]
        incoming.append(pltpu.make_async_copy(source, buf.at[n], sems.at[n]))
        outgoing.append(
            pltpu.make_async_copy(buf.at[n], out.at[n >> 1, j], sems.at[16 + n])
        )
    start_all(incoming)
    for one, two in zip(incoming, outgoing):
        one.wait()
        two.start()
    wait_all(outgoing)


def pack(base, i, rows, block):
    size = 8 * 2 * rows * block * 2
    return pl.pallas_call(
        functools.partial(pack_kernel, i, rows, block),
        out_shape=jax.ShapeDtypeStruct((8, 2, rows, block), BF16),
        in_specs=[ANY],
        out_specs=ANY,
        scratch_shapes=[
            pltpu.VMEM((16, rows, block), BF16),
            pltpu.SemaphoreType.DMA((32,)),
        ],
        compiler_params=pltpu.CompilerParams(vmem_limit_bytes=VMEM),
        cost_estimate=pl.CostEstimate(flops=0, bytes_accessed=2 * size, transcendentals=0),
    )(base)


def add_kernel(i, rows, block, picks, part, own, other, r0, r1, r2, r3, *refs):
    outs = refs[:8]
    lbuf, tbuf, rbuf, pbuf, obuf, sems = refs[8:]
    core = picks[32]
    copies = [pltpu.make_async_copy(part, pbuf, sems.at[8])]
    for n in range(8):
        for flip, source in ((0, own), (1, other)):
            lane = pl.multiple_of((core ^ flip) * rows, rows)
            copies.append(
                pltpu.make_async_copy(
                    source.at[n, :, :, pl.ds(i * rows, rows)],
                    lbuf.at[:, picks[24 + n], :, pl.ds(lane, rows)],
                    sems.at[9 + n * 2 + flip],
                )
            )
        source = (r0, r1, r2, r3)[n >> 1]
        for c in range(2):
            copies.append(
                pltpu.make_async_copy(
                    source.at[n & 1, c],
                    rbuf.at[:, :, picks[16 + n], c],
                    sems.at[25 + n * 2 + c],
                )
            )
    wait_all(start_all(copies))
    depth = 8 * lbuf.shape[2]
    for p in range(2):
        tbuf[p] = lbuf[p].reshape(depth, 2 * rows).T

    @pl.loop(0, 8)
    def _(k):
        y = picks[k]
        lanes = pl.ds(pl.multiple_of(picks[8 + k] * block, block), block)
        high, low = tbuf[0], tbuf[1]
        rhigh = rbuf[y, 0, :, :, :, lanes].reshape(depth, block)
        rlow = rbuf[y, 1, :, :, :, lanes].reshape(depth, block)
        dot = functools.partial(jnp.dot, preferred_element_type=jnp.float32)
        delta = dot(high, rhigh) + dot(high, rlow) + dot(low, rhigh)
        for c in range(2):
            stored = pbuf[c * 4 + y, picks[8 + k]].astype(jnp.float32)
            obuf[k, c] = (stored + delta[c * rows : (c + 1) * rows]).astype(BF16)

    wait_all(
        start_all(
            [pltpu.make_async_copy(obuf.at[k], outs[k], sems.at[k]) for k in range(8)]
        )
    )


def add(i, rows, block, picks, part, lefts, rights):
    depth = rights[0].shape[4]
    return pl.pallas_call(
        functools.partial(add_kernel, i, rows, block),
        out_shape=[jax.ShapeDtypeStruct((2, rows, block), BF16)] * 8,
        in_specs=[SMEM] + [ANY] * 7,
        out_specs=[ANY] * 8,
        scratch_shapes=[
            pltpu.VMEM((2, 8, lefts[0].shape[2], 2 * rows), BF16),
            pltpu.VMEM((2, 2 * rows, 8 * lefts[0].shape[2]), BF16),
            pltpu.VMEM((4, 2, 8, 2, depth, 2 * block), BF16),
            pltpu.VMEM((8, 2, rows, block), BF16),
            pltpu.VMEM((8, 2, rows, block), BF16),
            pltpu.SemaphoreType.DMA((41,)),
        ],
        compiler_params=pltpu.CompilerParams(vmem_limit_bytes=VMEM),
        cost_estimate=pl.CostEstimate(
            flops=2 * 16 * rows * block * 768, bytes_accessed=12 << 20, transcendentals=0
        ),
    )(picks, part, *lefts, *rights)


def place_kernel(i, rows, height, slots, *refs):
    got = refs[:8]
    out, buf, sems = refs[-3:]
    incoming, outgoing = [], []
    for k in range(8):
        incoming.append(pltpu.make_async_copy(got[k], buf.at[k], sems.at[k]))
        for c in range(2):
            start = (slots[k] * 2 + c) * height + i * rows
            outgoing.append(
                pltpu.make_async_copy(
                    buf.at[k, c],
                    out.at[pl.ds(pl.multiple_of(start, rows), rows)],
                    sems.at[8 + k * 2 + c],
                )
            )
    start_all(incoming)
    for k in range(8):
        incoming[k].wait()
        start_all(outgoing[2 * k : 2 * k + 2])
    wait_all(outgoing)


def place(i, rows, height, block, slots, got, merged):
    old = [] if merged is None else [merged]
    return pl.pallas_call(
        functools.partial(place_kernel, i, rows, height),
        out_shape=jax.ShapeDtypeStruct((16 * height, block), BF16),
        in_specs=[SMEM] + [ANY] * (8 + len(old)),
        out_specs=ANY,
        scratch_shapes=[
            pltpu.VMEM((8, 2, rows, block), BF16),
            pltpu.SemaphoreType.DMA((24,)),
        ],
        input_output_aliases={9: 0} if old else {},
        compiler_params=pltpu.CompilerParams(vmem_limit_bytes=VMEM),
        cost_estimate=pl.CostEstimate(
            flops=0, bytes_accessed=64 * rows * block, transcendentals=0
        ),
    )(slots, *got, *old)


def body(base, left, right):
    height, width = base.shape
    block = width // 16
    rows = height // CHUNKS
    depth, rank = right.shape[0], left.shape[1]
    z, xl, c, xh, y = (lax.axis_index(n) for n in AXES)
    tie = lax.optimization_barrier

    def across(value, change):
        return lax.ppermute(value, AXES, moved(change))

    rights = jnp.stack(split(right)).reshape(2, depth, 2, 2, 4, block)
    rights = rights.transpose(2, 4, 0, 1, 3, 5).reshape(8, 2 * depth, 2 * block)
    rights = lax.all_to_all(
        jnp.concatenate([rights, rights]), ("xl", "c", "y"), 0, 0, tiled=True
    ).reshape(2, 8, 2 * depth, 2 * block)
    lefts = jnp.stack(split(left.T))
    lefts = jnp.stack(
        [lefts]
        + [
            across(lefts, lambda z, xl, c, xh, y: (z, xl, c, xh, (y - d) % 4))
            for d in (1, 2, 3)
        ]
    )
    packed = [pack(base, i, rows, block) for i in range(CHUNKS)]
    packed[0], lefts, rights = tie((packed[0], lefts, rights))

    def first(i):
        return lax.all_to_all(packed[i], ("c", "y"), 0, 0, tiled=True)

    rights = [rights] + [
        across(rights, lambda z, xl, c, xh, y: ((z - d) % 4, xl, c, xh, y))
        for d in (1, 2, 3)
    ]
    rights = [one.reshape(2, 2, 4, 2, depth, 2 * block) for one in rights]
    far = across(lefts, lambda z, xl, c, xh, y: (z, xl, c, xh ^ 1, y))
    lefts = jnp.concatenate([lefts, far])
    lefts = [lefts, across(lefts, lambda z, xl, c, xh, y: (z, xl, c ^ 1, xh, y))]

    ys, js, zs, ls, slots = [], [], [], [], []
    for k in range(8):
        k2, k1, k0 = bits(k)
        ys.append(((z & 1) ^ k0) * 2 + (xl ^ k1))
        js.append((z >> 1) ^ k2 ^ c)
        zs.append(((z + (k >> 1)) & 3) * 2 + k0)
        ls.append((xh ^ k2) * 4 + ((y + (k & 3)) & 3))
        slots.append(((xh ^ k2 ^ c) * 2 + ((z & 1) ^ k0)) * 2 + (xl ^ k1))
    picks = jnp.stack([*ys, *js, *zs, *ls, c]).astype(jnp.int32)
    slots = jnp.stack(slots).astype(jnp.int32)

    merged = None
    arrived = first(0)
    packed[1], rights = tie((packed[1], rights))
    got, sent = [], add(0, rows, block, picks, arrived, lefts, rights)
    arrived = first(1)
    for i in range(CHUNKS):
        got, sent = tie((got, sent))
        new = [lax.ppermute(sent[k], AXES, pairs(k)) for k in range(8)]
        if got:
            merged = place(i - 1, rows, height, block, slots, got, merged)
        got = new
        if i + 1 < CHUNKS:
            landed = arrived
            if i + 2 < CHUNKS:
                packed[i + 2], landed, new[:AHEAD] = tie(
                    (packed[i + 2], landed, new[:AHEAD])
                )
                arrived = first(i + 2)
            sent = add(i + 1, rows, block, picks, landed, lefts, rights)
    return place(CHUNKS - 1, rows, height, block, slots, got, merged)


def solution(mesh):
    fine = Mesh(mesh.devices.reshape(SIZES), AXES)
    placed = P(("z", "xl", "c"), ("xh", "y"))
    return jax.shard_map(
        body,
        mesh=fine,
        in_specs=(placed, placed, placed),
        out_specs=P(None, AXES),
        check_vma=False,
    )
```

```python
import functools

import jax
import jax.numpy as jnp
from jax import lax
from jax.experimental import pallas as pl
from jax.experimental.pallas import tpu as pltpu
from jax.sharding import Mesh
from jax.sharding import PartitionSpec as P

AXES = ("z", "xl", "c", "xh", "y")
SIZES = (4, 2, 2, 2, 4)
CHUNKS = ((0, 256), (256, 384), (640, 384))
HALF = 4
ORDER = (0, 4, 1, 5, 2, 6, 3, 7)
AHEAD = 8
VMEM = 60 << 20
ANY = pl.BlockSpec(memory_space=pl.ANY)
SMEM = pl.BlockSpec(memory_space=pltpu.SMEM)
BF16 = jnp.bfloat16


def split(value):
    high = lax.reduce_precision(value, 8, 7)
    return high.astype(BF16), (value - high).astype(BF16)


def number(z, xl, c, xh, y):
    return (((z * 2 + xl) * 2 + c) * 2 + xh) * 4 + y


def bits(k):
    return k >> 2, (k >> 1) & 1, k & 1


def pairs(k):
    k2, k1, k0 = bits(k)
    out = []
    for z in range(4):
        for xl in range(2):
            for c in range(2):
                for xh in range(2):
                    for y in range(4):
                        xh2, xl2 = (z >> 1) ^ k2 ^ c, xl ^ k1
                        z2 = xh * 2 + ((z & 1) ^ k0)
                        out.append((number(z, xl, c, xh, y), number(z2, xl2, c, xh2, y)))
    return out


def moved(change):
    out = []
    for z in range(4):
        for xl in range(2):
            for c in range(2):
                for xh in range(2):
                    for y in range(4):
                        out.append((number(z, xl, c, xh, y), number(*change(z, xl, c, xh, y))))
    return out


def start_all(copies):
    for one in copies:
        one.start()
    return copies


def wait_all(copies):
    for one in copies:
        one.wait()


def pack_kernel(start, rows, block, base, out, buf, sems):
    incoming, outgoing = [], []
    for n in range(16):
        c, y, j = n >> 3, (n >> 1) & 3, n & 1
        column = (c * 8 + j * 4 + y) * block
        source = base.at[pl.ds(start, rows), pl.ds(column, block)]
        incoming.append(pltpu.make_async_copy(source, buf.at[n], sems.at[n]))
        outgoing.append(
            pltpu.make_async_copy(buf.at[n], out.at[n >> 1, j], sems.at[16 + n])
        )
    start_all(incoming)
    for one, two in zip(incoming, outgoing):
        one.wait()
        two.start()
    wait_all(outgoing)


def pack(base, start, rows, block):
    size = 8 * 2 * rows * block * 2
    return pl.pallas_call(
        functools.partial(pack_kernel, start, rows, block),
        out_shape=jax.ShapeDtypeStruct((8, 2, rows, block), BF16),
        in_specs=[ANY],
        out_specs=ANY,
        scratch_shapes=[
            pltpu.VMEM((16, rows, block), BF16),
            pltpu.SemaphoreType.DMA((32,)),
        ],
        compiler_params=pltpu.CompilerParams(vmem_limit_bytes=VMEM),
        cost_estimate=pl.CostEstimate(flops=0, bytes_accessed=2 * size, transcendentals=0),
    )(base)


def add_kernel(start, rows, block, first, picks, part, l0, l1, l2, l3, r0, r1, r2, r3, r4, *refs):
    outs = refs[:HALF]
    lbuf, tbuf, rbuf, pbuf, obuf, sems = refs[HALF:]
    core, low_bit = picks[32], picks[first] & 1
    copies = []
    for n in range(8):
        for flip, source in ((0, (l0, l1)), (1, (l2, l3))):
            lane = pl.multiple_of((core ^ flip) * rows, 128)
            copies.append(
                pltpu.make_async_copy(
                    source[n >> 2].at[n & 3, :, :, pl.ds(start, rows)],
                    lbuf.at[:, picks[24 + n], :, pl.ds(lane, rows)],
                    sems.at[n * 2 + flip],
                )
            )
        for c in range(2):
            copies.append(
                pltpu.make_async_copy(
                    (r0, r0, r1, r1, r2, r3, r4, r4)[n].at[
                        0 if n in (4, 5) else n & 1, c, :, low_bit
                    ],
                    rbuf.at[:, :, picks[16 + n], c],
                    sems.at[16 + n * 2 + c],
                )
            )
    stored = [
        pltpu.make_async_copy(
            part.at[c * 4 + picks[first + k], picks[8 + first + k]], pbuf.at[k * 2 + c], sems.at[32 + k * 2 + c]
        )
        for k in range(HALF)
        for c in range(2)
    ]
    start_all(copies + stored)
    wait_all(copies)
    depth = 8 * lbuf.shape[2]
    for p in range(2):
        tbuf[p] = lbuf[p].reshape(depth, 2 * rows).T
    dot = functools.partial(jnp.dot, preferred_element_type=jnp.float32)

    @pl.loop(0, HALF)
    def _(k):
        y = picks[first + k] >> 1
        lanes = pl.ds(pl.multiple_of(picks[8 + first + k] * block, block), block)
        rhigh = rbuf[y, 0, :, :, :, lanes].reshape(depth, block)
        rlow = rbuf[y, 1, :, :, :, lanes].reshape(depth, block)
        for c in range(2):
            n = k * 2 + c
            pltpu.make_async_copy(part.at[0, 0], pbuf.at[n], sems.at[32 + n]).wait()
            lines = pl.ds(c * rows, rows)
            high, low = tbuf[0, lines], tbuf[1, lines]
            delta = dot(high, rhigh) + dot(high, rlow) + dot(low, rhigh)
            obuf[k, c] = (pbuf[n].astype(jnp.float32) + delta).astype(BF16)

    wait_all(
        start_all(
            [pltpu.make_async_copy(obuf.at[k], outs[k], sems.at[k]) for k in range(HALF)]
        )
    )


def add(start, rows, block, first, picks, part, lefts, rights):
    depth = rights[0].shape[5]
    rank = lefts[0].shape[2]
    return pl.pallas_call(
        functools.partial(add_kernel, start, rows, block, first),
        out_shape=[jax.ShapeDtypeStruct((2, rows, block), BF16)] * HALF,
        in_specs=[SMEM] + [ANY] * 10,
        out_specs=[ANY] * HALF,
        scratch_shapes=[
            pltpu.VMEM((2, 8, rank, 2 * rows), BF16),
            pltpu.VMEM((2, 2 * rows, 8 * rank), BF16),
            pltpu.VMEM((2, 2, 8, 2, depth, 2 * block), BF16),
            pltpu.VMEM((8, rows, block), BF16),
            pltpu.VMEM((HALF, 2, rows, block), BF16),
            pltpu.SemaphoreType.DMA((40,)),
        ],
        compiler_params=pltpu.CompilerParams(vmem_limit_bytes=VMEM),
        cost_estimate=pl.CostEstimate(
            flops=2 * 8 * rows * block * 768, bytes_accessed=8 << 20, transcendentals=0
        ),
    )(picks, part, *lefts, *rights)


def place_kernel(start, rows, height, first, slots, *refs):
    got = refs[:HALF]
    out, buf, sems = refs[-3:]
    incoming, outgoing = [], []
    for k in range(HALF):
        incoming.append(pltpu.make_async_copy(got[k], buf.at[k], sems.at[k]))
        for c in range(2):
            row = (slots[first + k] * 2 + c) * height + start
            outgoing.append(
                pltpu.make_async_copy(
                    buf.at[k, c],
                    out.at[pl.ds(pl.multiple_of(row, 128), rows)],
                    sems.at[HALF + k * 2 + c],
                )
            )
    start_all(incoming)
    for k in range(HALF):
        incoming[k].wait()
        start_all(outgoing[2 * k : 2 * k + 2])
    wait_all(outgoing)


def place(start, rows, height, block, first, slots, got, merged):
    old = [] if merged is None else [merged]
    return pl.pallas_call(
        functools.partial(place_kernel, start, rows, height, first),
        out_shape=jax.ShapeDtypeStruct((16 * height, block), BF16),
        in_specs=[SMEM] + [ANY] * (HALF + len(old)),
        out_specs=ANY,
        scratch_shapes=[
            pltpu.VMEM((HALF, 2, rows, block), BF16),
            pltpu.SemaphoreType.DMA((3 * HALF,)),
        ],
        input_output_aliases={HALF + 1: 0} if old else {},
        compiler_params=pltpu.CompilerParams(vmem_limit_bytes=VMEM),
        cost_estimate=pl.CostEstimate(
            flops=0, bytes_accessed=32 * rows * block, transcendentals=0
        ),
    )(slots, *got, *old)


def body(base, left, right):
    height, width = base.shape
    block = width // 16
    depth, rank = right.shape[0], left.shape[1]
    z, xl, c, xh, y = (lax.axis_index(n) for n in AXES)
    tie = lax.optimization_barrier

    def across(value, change):
        return lax.ppermute(value, AXES, moved(change))

    rights = jnp.stack(split(right)).reshape(2, depth, 2, 2, 4, block)
    rights = rights.transpose(2, 4, 0, 1, 3, 5).reshape(8, 2 * depth, 2 * block)
    rights = lax.all_to_all(
        jnp.concatenate([rights, rights]), ("xl", "c", "y"), 0, 0, tiled=True
    ).reshape(2, 8, 2 * depth, 2 * block)
    lefts = jnp.stack(split(left.T))
    lefts = jnp.stack(
        [lefts]
        + [
            across(lefts, lambda z, xl, c, xh, y: (z, xl, c, xh, (y - d) % 4))
            for d in (1, 2, 3)
        ]
    )
    packed = [pack(base, *chunk, block) for chunk in CHUNKS]
    packed[0], lefts, rights = tie((packed[0], lefts, rights))

    def first(i):
        return lax.all_to_all(packed[i], ("c", "y"), 0, 0, tiled=True)

    def down(value):
        return across(value, lambda z, xl, c, xh, y: ((z - 1) % 4, xl, c, xh, y))

    def up(value):
        return across(value, lambda z, xl, c, xh, y: ((z + 1) % 4, xl, c, xh, y))

    above, below = down(rights), up(rights)
    rights = [rights, above, down(above[:1]), up(below[1:]), below]
    rights = [one.reshape(-1, 2, 2, 2, 2, depth, 2 * block) for one in rights]
    lefts = [
        lefts,
        across(lefts, lambda z, xl, c, xh, y: (z, xl, c, xh ^ 1, y)),
        across(lefts, lambda z, xl, c, xh, y: (z, xl, c ^ 1, xh, y)),
        across(lefts, lambda z, xl, c, xh, y: (z, xl, c ^ 1, xh ^ 1, y)),
    ]

    ys, js, zs, ls, slots = [], [], [], [], []
    for n in range(8):
        zs.append(((z + (n >> 1)) & 3) * 2 + (n & 1))
        ls.append((xh ^ (n >> 2)) * 4 + ((y + (n & 3)) & 3))
        k2, k1, k0 = bits(ORDER[n])
        ys.append(((z & 1) ^ k0) * 2 + (xl ^ k1))
        js.append((z >> 1) ^ k2 ^ c)
        slots.append(((xh ^ k2 ^ c) * 2 + ((z & 1) ^ k0)) * 2 + (xl ^ k1))
    picks = jnp.stack([*ys, *js, *zs, *ls, c]).astype(jnp.int32)
    slots = jnp.stack(slots).astype(jnp.int32)

    merged = None
    landed = first(0)

    def total(s, part):
        return [
            one
            for half in (0, HALF)
            for one in add(*CHUNKS[s], block, half, picks, part, lefts, rights)
        ]

    def finish(s, got, merged):
        for half in (0, HALF):
            merged = place(
                *CHUNKS[s], height, block, half, slots, got[half : half + HALF], merged
            )
        return merged

    count = len(CHUNKS)
    packed[1], lefts, rights = tie((packed[1], lefts, rights))
    got, sent = [], total(0, landed)
    arrived = first(1)
    for s in range(count):
        if s:
            got, sent[:HALF] = tie((got, sent[:HALF]))
        new = []
        for k in range(8):
            if k == HALF:
                new[0], sent[HALF:] = tie((new[0], sent[HALF:]))
            new.append(lax.ppermute(sent[k], AXES, pairs(ORDER[k])))
        if got:
            merged = finish(s - 1, got, merged)
        if s + 1 < count:
            landed = arrived
            if s + 2 < count:
                packed[s + 2] = tie((packed[s + 2], landed, new[:AHEAD]))[0]
                arrived = first(s + 2)
            sent = total(s + 1, landed)
        got = new
    return finish(count - 1, got, merged)


def solution(mesh):
    fine = Mesh(mesh.devices.reshape(SIZES), AXES)
    placed = P(("z", "xl", "c"), ("xh", "y"))
    return jax.shard_map(
        body,
        mesh=fine,
        in_specs=(placed, placed, placed),
        out_specs=P(None, AXES),
        check_vma=False,
    )
```

```python
import functools

import jax
import jax.numpy as jnp
from jax import lax
from jax.experimental import pallas as pl
from jax.experimental.pallas import tpu as pltpu
from jax.sharding import Mesh
from jax.sharding import PartitionSpec as P

AXES = ("z", "xl", "c", "xh", "y")
SIZES = (4, 2, 2, 2, 4)
CHUNKS = ((0, 256), (256, 384), (640, 384))
HALF = 4
EARLY = 4
ORDER = (0, 4, 1, 5, 2, 6, 3, 7)
AHEAD = 8
VMEM = 60 << 20
ANY = pl.BlockSpec(memory_space=pl.ANY)
SMEM = pl.BlockSpec(memory_space=pltpu.SMEM)
BF16 = jnp.bfloat16


def split(value):
    high = lax.reduce_precision(value, 8, 7)
    return high.astype(BF16), (value - high).astype(BF16)


def number(z, xl, c, xh, y):
    return (((z * 2 + xl) * 2 + c) * 2 + xh) * 4 + y


def bits(k):
    return k >> 2, (k >> 1) & 1, k & 1


def pairs(k):
    k2, k1, k0 = bits(k)
    out = []
    for z in range(4):
        for xl in range(2):
            for c in range(2):
                for xh in range(2):
                    for y in range(4):
                        xh2, xl2 = (z >> 1) ^ k2 ^ c, xl ^ k1
                        z2 = xh * 2 + ((z & 1) ^ k0)
                        out.append((number(z, xl, c, xh, y), number(z2, xl2, c, xh2, y)))
    return out


def moved(change):
    out = []
    for z in range(4):
        for xl in range(2):
            for c in range(2):
                for xh in range(2):
                    for y in range(4):
                        out.append((number(z, xl, c, xh, y), number(*change(z, xl, c, xh, y))))
    return out


def start_all(copies):
    for one in copies:
        one.start()
    return copies


def wait_all(copies):
    for one in copies:
        one.wait()


def pack_kernel(start, rows, block, base, out, buf, sems):
    incoming, outgoing = [], []
    for n in range(16):
        c, y, j = n >> 3, (n >> 1) & 3, n & 1
        column = (c * 8 + j * 4 + y) * block
        source = base.at[pl.ds(start, rows), pl.ds(column, block)]
        incoming.append(pltpu.make_async_copy(source, buf.at[n], sems.at[n]))
        outgoing.append(
            pltpu.make_async_copy(buf.at[n], out.at[n >> 1, j], sems.at[16 + n])
        )
    start_all(incoming)
    for one, two in zip(incoming, outgoing):
        one.wait()
        two.start()
    wait_all(outgoing)


def pack(base, start, rows, block):
    size = 8 * 2 * rows * block * 2
    return pl.pallas_call(
        functools.partial(pack_kernel, start, rows, block),
        out_shape=jax.ShapeDtypeStruct((8, 2, rows, block), BF16),
        in_specs=[ANY],
        out_specs=ANY,
        scratch_shapes=[
            pltpu.VMEM((16, rows, block), BF16),
            pltpu.SemaphoreType.DMA((32,)),
        ],
        compiler_params=pltpu.CompilerParams(vmem_limit_bytes=VMEM),
        cost_estimate=pl.CostEstimate(flops=0, bytes_accessed=2 * size, transcendentals=0),
    )(base)


def add_kernel(start, rows, block, first, picks, part, l0, l1, l2, l3, r0, r1, r2, r3, r4, *refs):
    outs = refs[:HALF]
    lbuf, tbuf, rbuf, pbuf, obuf, sems = refs[HALF:]
    core, low_bit = picks[32], picks[first] & 1
    copies = []
    for n in range(8):
        for flip, source in ((0, (l0, l1)), (1, (l2, l3))):
            lane = pl.multiple_of((core ^ flip) * rows, 128)
            copies.append(
                pltpu.make_async_copy(
                    source[n >> 2].at[n & 3, :, :, pl.ds(start, rows)],
                    lbuf.at[:, picks[24 + n], :, pl.ds(lane, rows)],
                    sems.at[n * 2 + flip],
                )
            )
        for c in range(2):
            copies.append(
                pltpu.make_async_copy(
                    (r0, r0, r1, r1, r2, r3, r4, r4)[n].at[
                        0 if n in (4, 5) else n & 1, c, :, low_bit
                    ],
                    rbuf.at[:, :, picks[16 + n], c],
                    sems.at[16 + n * 2 + c],
                )
            )
    stored = [
        pltpu.make_async_copy(
            part.at[c * 4 + picks[first + k], picks[8 + first + k]], pbuf.at[k * 2 + c], sems.at[32 + k * 2 + c]
        )
        for k in range(HALF)
        for c in range(2)
    ]
    start_all(copies + stored)
    wait_all(copies)
    depth = 8 * lbuf.shape[2]
    for p in range(2):
        tbuf[p] = lbuf[p].reshape(depth, 2 * rows).T
    dot = functools.partial(jnp.dot, preferred_element_type=jnp.float32)

    @pl.loop(0, HALF)
    def _(k):
        y = picks[first + k] >> 1
        lanes = pl.ds(pl.multiple_of(picks[8 + first + k] * block, block), block)
        rhigh = rbuf[y, 0, :, :, :, lanes].reshape(depth, block)
        rlow = rbuf[y, 1, :, :, :, lanes].reshape(depth, block)
        for c in range(2):
            n = k * 2 + c
            pltpu.make_async_copy(part.at[0, 0], pbuf.at[n], sems.at[32 + n]).wait()
            lines = pl.ds(c * rows, rows)
            high, low = tbuf[0, lines], tbuf[1, lines]
            delta = dot(high, rhigh) + dot(high, rlow) + dot(low, rhigh)
            obuf[k, c] = (pbuf[n].astype(jnp.float32) + delta).astype(BF16)

    wait_all(
        start_all(
            [pltpu.make_async_copy(obuf.at[k], outs[k], sems.at[k]) for k in range(HALF)]
        )
    )


def add(start, rows, block, first, picks, part, lefts, rights):
    depth = rights[0].shape[5]
    rank = lefts[0].shape[2]
    return pl.pallas_call(
        functools.partial(add_kernel, start, rows, block, first),
        out_shape=[jax.ShapeDtypeStruct((2, rows, block), BF16)] * HALF,
        in_specs=[SMEM] + [ANY] * 10,
        out_specs=[ANY] * HALF,
        scratch_shapes=[
            pltpu.VMEM((2, 8, rank, 2 * rows), BF16),
            pltpu.VMEM((2, 2 * rows, 8 * rank), BF16),
            pltpu.VMEM((2, 2, 8, 2, depth, 2 * block), BF16),
            pltpu.VMEM((8, rows, block), BF16),
            pltpu.VMEM((HALF, 2, rows, block), BF16),
            pltpu.SemaphoreType.DMA((40,)),
        ],
        compiler_params=pltpu.CompilerParams(vmem_limit_bytes=VMEM),
        cost_estimate=pl.CostEstimate(
            flops=2 * 8 * rows * block * 768, bytes_accessed=8 << 20, transcendentals=0
        ),
    )(picks, part, *lefts, *rights)


def place_kernel(start, rows, height, first, slots, *refs):
    got = refs[:HALF]
    out, buf, sems = refs[-3:]
    incoming, outgoing = [], []
    for k in range(HALF):
        incoming.append(pltpu.make_async_copy(got[k], buf.at[k], sems.at[k]))
        for c in range(2):
            row = (slots[first + k] * 2 + c) * height + start
            outgoing.append(
                pltpu.make_async_copy(
                    buf.at[k, c],
                    out.at[pl.ds(pl.multiple_of(row, 128), rows)],
                    sems.at[HALF + k * 2 + c],
                )
            )
    start_all(incoming)
    for k in range(HALF):
        incoming[k].wait()
        start_all(outgoing[2 * k : 2 * k + 2])
    wait_all(outgoing)


def place(start, rows, height, block, first, slots, got, merged):
    old = [] if merged is None else [merged]
    return pl.pallas_call(
        functools.partial(place_kernel, start, rows, height, first),
        out_shape=jax.ShapeDtypeStruct((16 * height, block), BF16),
        in_specs=[SMEM] + [ANY] * (HALF + len(old)),
        out_specs=ANY,
        scratch_shapes=[
            pltpu.VMEM((HALF, 2, rows, block), BF16),
            pltpu.SemaphoreType.DMA((3 * HALF,)),
        ],
        input_output_aliases={HALF + 1: 0} if old else {},
        compiler_params=pltpu.CompilerParams(vmem_limit_bytes=VMEM),
        cost_estimate=pl.CostEstimate(
            flops=0, bytes_accessed=32 * rows * block, transcendentals=0
        ),
    )(slots, *got, *old)


def body(base, left, right):
    height, width = base.shape
    block = width // 16
    depth, rank = right.shape[0], left.shape[1]
    z, xl, c, xh, y = (lax.axis_index(n) for n in AXES)
    tie = lax.optimization_barrier

    def across(value, change):
        return lax.ppermute(value, AXES, moved(change))

    rights = jnp.stack(split(right)).reshape(2, depth, 2, 2, 4, block)
    rights = rights.transpose(2, 4, 0, 1, 3, 5).reshape(8, 2 * depth, 2 * block)
    rights = lax.all_to_all(
        jnp.concatenate([rights, rights]), ("xl", "c", "y"), 0, 0, tiled=True
    ).reshape(2, 8, 2 * depth, 2 * block)
    lefts = jnp.stack(split(left.T))
    lefts = jnp.stack(
        [lefts]
        + [
            across(lefts, lambda z, xl, c, xh, y: (z, xl, c, xh, (y - d) % 4))
            for d in (1, 2, 3)
        ]
    )
    packed = [pack(base, *chunk, block) for chunk in CHUNKS]
    packed[0], lefts, rights = tie((packed[0], lefts, rights))

    def first(i):
        return lax.all_to_all(packed[i], ("c", "y"), 0, 0, tiled=True)

    def down(value):
        return across(value, lambda z, xl, c, xh, y: ((z - 1) % 4, xl, c, xh, y))

    def up(value):
        return across(value, lambda z, xl, c, xh, y: ((z + 1) % 4, xl, c, xh, y))

    above, below = down(rights), up(rights)
    rights = [rights, above, down(above[:1]), up(below[1:]), below]
    rights = [one.reshape(-1, 2, 2, 2, 2, depth, 2 * block) for one in rights]
    lefts = [
        lefts,
        across(lefts, lambda z, xl, c, xh, y: (z, xl, c, xh ^ 1, y)),
        across(lefts, lambda z, xl, c, xh, y: (z, xl, c ^ 1, xh, y)),
        across(lefts, lambda z, xl, c, xh, y: (z, xl, c ^ 1, xh ^ 1, y)),
    ]

    ys, js, zs, ls, slots = [], [], [], [], []
    for n in range(8):
        zs.append(((z + (n >> 1)) & 3) * 2 + (n & 1))
        ls.append((xh ^ (n >> 2)) * 4 + ((y + (n & 3)) & 3))
        k2, k1, k0 = bits(ORDER[n])
        ys.append(((z & 1) ^ k0) * 2 + (xl ^ k1))
        js.append((z >> 1) ^ k2 ^ c)
        slots.append(((xh ^ k2 ^ c) * 2 + ((z & 1) ^ k0)) * 2 + (xl ^ k1))
    picks = jnp.stack([*ys, *js, *zs, *ls, c]).astype(jnp.int32)
    slots = jnp.stack(slots).astype(jnp.int32)

    merged = None
    landed = first(0)

    def total(s, part):
        return [
            one
            for half in (0, HALF)
            for one in add(*CHUNKS[s], block, half, picks, part, lefts, rights)
        ]

    def finish(s, got, merged):
        for half in (0, HALF):
            merged = place(
                *CHUNKS[s], height, block, half, slots, got[half : half + HALF], merged
            )
        return merged

    count = len(CHUNKS)
    packed[1], lefts, rights = tie((packed[1], lefts, rights))
    got, sent = [], total(0, landed)
    arrived = first(1)
    for s in range(count):
        if s:
            got[:EARLY], sent[:HALF] = tie((got[:EARLY], sent[:HALF]))
        new = []
        for k in range(8):
            if k == HALF:
                new[0], got[EARLY:], sent[HALF:] = tie(
                    (new[0], got[EARLY:], sent[HALF:])
                )
            new.append(lax.ppermute(sent[k], AXES, pairs(ORDER[k])))
        if got:
            merged = finish(s - 1, got, merged)
        if s + 1 < count:
            landed = arrived
            if s + 2 < count:
                packed[s + 2] = tie((packed[s + 2], landed, new[:AHEAD]))[0]
                arrived = first(s + 2)
            sent = total(s + 1, landed)
        got = new
    return finish(count - 1, got, merged)


def solution(mesh):
    fine = Mesh(mesh.devices.reshape(SIZES), AXES)
    placed = P(("z", "xl", "c"), ("xh", "y"))
    return jax.shard_map(
        body,
        mesh=fine,
        in_specs=(placed, placed, placed),
        out_specs=P(None, AXES),
        check_vma=False,
    )
```

```python
import functools

import jax
import jax.numpy as jnp
from jax import lax
from jax.experimental import pallas as pl
from jax.experimental.pallas import tpu as pltpu
from jax.sharding import Mesh
from jax.sharding import PartitionSpec as P

AXES = ("z", "xl", "c", "xh", "y")
SIZES = (4, 2, 2, 2, 4)
CHUNKS = ((0, 256), (256, 384), (640, 384))
HALF = 4
EARLY = 2
ORDER = (0, 4, 1, 5, 2, 6, 3, 7)
AHEAD = 8
VMEM = 60 << 20
ANY = pl.BlockSpec(memory_space=pl.ANY)
SMEM = pl.BlockSpec(memory_space=pltpu.SMEM)
BF16 = jnp.bfloat16


def split(value):
    high = lax.reduce_precision(value, 8, 7)
    return high.astype(BF16), (value - high).astype(BF16)


def number(z, xl, c, xh, y):
    return (((z * 2 + xl) * 2 + c) * 2 + xh) * 4 + y


def bits(k):
    return k >> 2, (k >> 1) & 1, k & 1


def pairs(k):
    k2, k1, k0 = bits(k)
    out = []
    for z in range(4):
        for xl in range(2):
            for c in range(2):
                for xh in range(2):
                    for y in range(4):
                        xh2, xl2 = (z >> 1) ^ k2 ^ c, xl ^ k1
                        z2 = xh * 2 + ((z & 1) ^ k0)
                        out.append((number(z, xl, c, xh, y), number(z2, xl2, c, xh2, y)))
    return out


def moved(change):
    out = []
    for z in range(4):
        for xl in range(2):
            for c in range(2):
                for xh in range(2):
                    for y in range(4):
                        out.append((number(z, xl, c, xh, y), number(*change(z, xl, c, xh, y))))
    return out


def start_all(copies):
    for one in copies:
        one.start()
    return copies


def wait_all(copies):
    for one in copies:
        one.wait()


def pack_kernel(start, rows, block, base, out, buf, sems):
    incoming, outgoing = [], []
    for n in range(16):
        c, y, j = n >> 3, (n >> 1) & 3, n & 1
        column = (c * 8 + j * 4 + y) * block
        source = base.at[pl.ds(start, rows), pl.ds(column, block)]
        incoming.append(pltpu.make_async_copy(source, buf.at[n], sems.at[n]))
        outgoing.append(
            pltpu.make_async_copy(buf.at[n], out.at[n >> 1, j], sems.at[16 + n])
        )
    start_all(incoming)
    for one, two in zip(incoming, outgoing):
        one.wait()
        two.start()
    wait_all(outgoing)


def pack(base, start, rows, block):
    size = 8 * 2 * rows * block * 2
    return pl.pallas_call(
        functools.partial(pack_kernel, start, rows, block),
        out_shape=jax.ShapeDtypeStruct((8, 2, rows, block), BF16),
        in_specs=[ANY],
        out_specs=ANY,
        scratch_shapes=[
            pltpu.VMEM((16, rows, block), BF16),
            pltpu.SemaphoreType.DMA((32,)),
        ],
        compiler_params=pltpu.CompilerParams(vmem_limit_bytes=VMEM),
        cost_estimate=pl.CostEstimate(flops=0, bytes_accessed=2 * size, transcendentals=0),
    )(base)


def add_kernel(start, rows, block, first, picks, part, l0, l1, l2, l3, r0, r1, r2, r3, r4, *refs):
    outs = refs[:HALF]
    lbuf, tbuf, rbuf, pbuf, obuf, sems = refs[HALF:]
    core, low_bit = picks[32], picks[first] & 1
    copies = []
    for n in range(8):
        for flip, source in ((0, (l0, l1)), (1, (l2, l3))):
            lane = pl.multiple_of((core ^ flip) * rows, 128)
            copies.append(
                pltpu.make_async_copy(
                    source[n >> 2].at[n & 3, :, :, pl.ds(start, rows)],
                    lbuf.at[:, picks[24 + n], :, pl.ds(lane, rows)],
                    sems.at[n * 2 + flip],
                )
            )
        for c in range(2):
            copies.append(
                pltpu.make_async_copy(
                    (r0, r0, r1, r1, r2, r3, r4, r4)[n].at[
                        0 if n in (4, 5) else n & 1, c, :, low_bit
                    ],
                    rbuf.at[:, :, picks[16 + n], c],
                    sems.at[16 + n * 2 + c],
                )
            )
    stored = [
        pltpu.make_async_copy(
            part.at[c * 4 + picks[first + k], picks[8 + first + k]], pbuf.at[k * 2 + c], sems.at[32 + k * 2 + c]
        )
        for k in range(HALF)
        for c in range(2)
    ]
    start_all(copies + stored)
    wait_all(copies)
    depth = 8 * lbuf.shape[2]
    for p in range(2):
        tbuf[p] = lbuf[p].reshape(depth, 2 * rows).T
    dot = functools.partial(jnp.dot, preferred_element_type=jnp.float32)

    @pl.loop(0, HALF)
    def _(k):
        y = picks[first + k] >> 1
        lanes = pl.ds(pl.multiple_of(picks[8 + first + k] * block, block), block)
        rhigh = rbuf[y, 0, :, :, :, lanes].reshape(depth, block)
        rlow = rbuf[y, 1, :, :, :, lanes].reshape(depth, block)
        for c in range(2):
            n = k * 2 + c
            pltpu.make_async_copy(part.at[0, 0], pbuf.at[n], sems.at[32 + n]).wait()
            lines = pl.ds(c * rows, rows)
            high, low = tbuf[0, lines], tbuf[1, lines]
            delta = dot(high, rhigh) + dot(high, rlow) + dot(low, rhigh)
            obuf[k, c] = (pbuf[n].astype(jnp.float32) + delta).astype(BF16)

    wait_all(
        start_all(
            [pltpu.make_async_copy(obuf.at[k], outs[k], sems.at[k]) for k in range(HALF)]
        )
    )


def add(start, rows, block, first, picks, part, lefts, rights):
    depth = rights[0].shape[5]
    rank = lefts[0].shape[2]
    return pl.pallas_call(
        functools.partial(add_kernel, start, rows, block, first),
        out_shape=[jax.ShapeDtypeStruct((2, rows, block), BF16)] * HALF,
        in_specs=[SMEM] + [ANY] * 10,
        out_specs=[ANY] * HALF,
        scratch_shapes=[
            pltpu.VMEM((2, 8, rank, 2 * rows), BF16),
            pltpu.VMEM((2, 2 * rows, 8 * rank), BF16),
            pltpu.VMEM((2, 2, 8, 2, depth, 2 * block), BF16),
            pltpu.VMEM((8, rows, block), BF16),
            pltpu.VMEM((HALF, 2, rows, block), BF16),
            pltpu.SemaphoreType.DMA((40,)),
        ],
        compiler_params=pltpu.CompilerParams(vmem_limit_bytes=VMEM),
        cost_estimate=pl.CostEstimate(
            flops=2 * 8 * rows * block * 768, bytes_accessed=8 << 20, transcendentals=0
        ),
    )(picks, part, *lefts, *rights)


def place_kernel(start, rows, height, first, slots, *refs):
    got = refs[:HALF]
    out, buf, sems = refs[-3:]
    incoming, outgoing = [], []
    for k in range(HALF):
        incoming.append(pltpu.make_async_copy(got[k], buf.at[k], sems.at[k]))
        for c in range(2):
            row = (slots[first + k] * 2 + c) * height + start
            outgoing.append(
                pltpu.make_async_copy(
                    buf.at[k, c],
                    out.at[pl.ds(pl.multiple_of(row, 128), rows)],
                    sems.at[HALF + k * 2 + c],
                )
            )
    start_all(incoming)
    for k in range(HALF):
        incoming[k].wait()
        start_all(outgoing[2 * k : 2 * k + 2])
    wait_all(outgoing)


def place(start, rows, height, block, first, slots, got, merged):
    old = [] if merged is None else [merged]
    return pl.pallas_call(
        functools.partial(place_kernel, start, rows, height, first),
        out_shape=jax.ShapeDtypeStruct((16 * height, block), BF16),
        in_specs=[SMEM] + [ANY] * (HALF + len(old)),
        out_specs=ANY,
        scratch_shapes=[
            pltpu.VMEM((HALF, 2, rows, block), BF16),
            pltpu.SemaphoreType.DMA((3 * HALF,)),
        ],
        input_output_aliases={HALF + 1: 0} if old else {},
        compiler_params=pltpu.CompilerParams(vmem_limit_bytes=VMEM),
        cost_estimate=pl.CostEstimate(
            flops=0, bytes_accessed=32 * rows * block, transcendentals=0
        ),
    )(slots, *got, *old)


def body(base, left, right):
    height, width = base.shape
    block = width // 16
    depth, rank = right.shape[0], left.shape[1]
    z, xl, c, xh, y = (lax.axis_index(n) for n in AXES)
    tie = lax.optimization_barrier

    def across(value, change):
        return lax.ppermute(value, AXES, moved(change))

    rights = jnp.stack(split(right)).reshape(2, depth, 2, 2, 4, block)
    rights = rights.transpose(2, 4, 0, 1, 3, 5).reshape(8, 2 * depth, 2 * block)
    rights = lax.all_to_all(
        jnp.concatenate([rights, rights]), ("xl", "c", "y"), 0, 0, tiled=True
    ).reshape(2, 8, 2 * depth, 2 * block)
    lefts = jnp.stack(split(left.T))
    lefts = jnp.stack(
        [lefts]
        + [
            across(lefts, lambda z, xl, c, xh, y: (z, xl, c, xh, (y - d) % 4))
            for d in (1, 2, 3)
        ]
    )
    packed = [pack(base, *chunk, block) for chunk in CHUNKS]
    packed[0], lefts, rights = tie((packed[0], lefts, rights))

    def first(i):
        return lax.all_to_all(packed[i], ("c", "y"), 0, 0, tiled=True)

    def down(value):
        return across(value, lambda z, xl, c, xh, y: ((z - 1) % 4, xl, c, xh, y))

    def up(value):
        return across(value, lambda z, xl, c, xh, y: ((z + 1) % 4, xl, c, xh, y))

    above, below = down(rights), up(rights)
    rights = [rights, above, down(above[:1]), up(below[1:]), below]
    rights = [one.reshape(-1, 2, 2, 2, 2, depth, 2 * block) for one in rights]
    lefts = [
        lefts,
        across(lefts, lambda z, xl, c, xh, y: (z, xl, c, xh ^ 1, y)),
        across(lefts, lambda z, xl, c, xh, y: (z, xl, c ^ 1, xh, y)),
        across(lefts, lambda z, xl, c, xh, y: (z, xl, c ^ 1, xh ^ 1, y)),
    ]

    ys, js, zs, ls, slots = [], [], [], [], []
    for n in range(8):
        zs.append(((z + (n >> 1)) & 3) * 2 + (n & 1))
        ls.append((xh ^ (n >> 2)) * 4 + ((y + (n & 3)) & 3))
        k2, k1, k0 = bits(ORDER[n])
        ys.append(((z & 1) ^ k0) * 2 + (xl ^ k1))
        js.append((z >> 1) ^ k2 ^ c)
        slots.append(((xh ^ k2 ^ c) * 2 + ((z & 1) ^ k0)) * 2 + (xl ^ k1))
    picks = jnp.stack([*ys, *js, *zs, *ls, c]).astype(jnp.int32)
    slots = jnp.stack(slots).astype(jnp.int32)

    merged = None
    landed = first(0)

    def total(s, part):
        return [
            one
            for half in (0, HALF)
            for one in add(*CHUNKS[s], block, half, picks, part, lefts, rights)
        ]

    def finish(s, got, merged):
        for half in (0, HALF):
            merged = place(
                *CHUNKS[s], height, block, half, slots, got[half : half + HALF], merged
            )
        return merged

    count = len(CHUNKS)
    packed[1], lefts, rights = tie((packed[1], lefts, rights))
    got, sent = [], total(0, landed)
    arrived = first(1)
    for s in range(count):
        if s:
            got[:EARLY], sent[:HALF] = tie((got[:EARLY], sent[:HALF]))
        new = []
        for k in range(8):
            if k == HALF:
                new[0], got[EARLY:], sent[HALF:] = tie(
                    (new[0], got[EARLY:], sent[HALF:])
                )
            new.append(lax.ppermute(sent[k], AXES, pairs(ORDER[k])))
        if got:
            merged = finish(s - 1, got, merged)
        if s + 1 < count:
            landed = arrived
            if s + 2 < count:
                packed[s + 2] = tie((packed[s + 2], landed, new[:AHEAD]))[0]
                arrived = first(s + 2)
            sent = total(s + 1, landed)
        got = new
    return finish(count - 1, got, merged)


def solution(mesh):
    fine = Mesh(mesh.devices.reshape(SIZES), AXES)
    placed = P(("z", "xl", "c"), ("xh", "y"))
    return jax.shard_map(
        body,
        mesh=fine,
        in_specs=(placed, placed, placed),
        out_specs=P(None, AXES),
        check_vma=False,
    )
```
